32 devices in a mesh: seq: 16 (over z, y, x), head: 2 (over core).
Axes of the slice: x: 2, y: 2, z: 4, core: 2. Of those that a mesh axis runs over, the one named last changes fastest.
Arguments:
- queries: bfloat16 [4096, 768], P('seq', 'head'), may hold values from -160 to 160
- keys: bfloat16 [4096, 768], P('seq', 'head'), may hold values from -40 to 40
- values: bfloat16 [4096, 768], P('seq', 'head'), may hold values from -6 to 6
- token_perm: int32 [6, 4096], P('head'), may hold values from 0 to 4095, as said below
- pair_blocks: int32 [6, 64, 4], P('head', 'seq'), may hold values from 0 to 63, as said below
- pair_counts: int32 [6, 64], P('head', 'seq'), may hold values from 2 to 4
- out_weight: bfloat16 [768, 5120], P('head'), may hold values from -0.875 to 0.875
Outputs:
- layer_out: bfloat16 [4096, 5120], P('seq', 'head')
The draws below stay inside these ranges and needn't reach their ends.
Inputs may be any that keep to these rules, and one draw needn't show every extreme that they name: Each row token_perm[h] is a permutation of the tokens 0 to 4095; position p belongs to index p // 256 of seq. Of the tokens of one index of seq, at most 32 take positions of any one index, for every head. pair_blocks[h, b, r] is a key block of head h for query block b; the 4 entries of one list are distinct. Block c belongs to index c // 4 of seq. All entries, live or not, of the 4 query blocks of one index of seq name at most one block of any other index and none of their own. The first pair_counts[h, b] entries of pair_blocks[h, b] are live; the others are not visible.
All inputs are finite; a program needn't handle non-finite values.
Results may differ from the reference program's by a relative error of at most 0.013.
Values may be sent and summed in bfloat16 or wider, within the bound.
A program may use at most 64 MiB of HBM per device.

```python
import math
import jax
import jax.numpy as jnp
from jax import lax

D = 5120
HEAD_SIZE = 128
HEADS_DEV = 3
BLOCKS_DEV = 4
TOK_DEV = 256
TOKENS = 4096
HEADS = 6
BLOCK_POSITIONS = 64
HEAD_BLOCKS = 64
LISTED_KEY_BLOCKS = 4
CAP = 32
N_SEQ = 16
N_HEAD = 2


def perm_table(key):
    base_key = jax.random.fold_in(key, 101)

    def one_head(head_key):
        lot_sizes = jnp.concatenate([jnp.full((N_SEQ // 4,), CAP, jnp.int32), jnp.full((N_SEQ // 2,), CAP // 2, jnp.int32), jnp.zeros((N_SEQ - N_SEQ // 4 - N_SEQ // 2,), jnp.int32)])
        lot_sizes = jax.random.permutation(jax.random.fold_in(head_key, 1), lot_sizes)
        lot_ends = jnp.cumsum(lot_sizes)
        slot_index = jnp.arange(TOK_DEV, dtype=jnp.int32)
        lot_of_slot = jnp.sum((lot_ends[None, :] <= slot_index[:, None]).astype(jnp.int32), axis=1)
        source_keys = jax.random.split(jax.random.fold_in(head_key, 2), N_SEQ)
        target_keys = jax.random.split(jax.random.fold_in(head_key, 3), N_SEQ)
        source_order = jax.vmap(lambda sub_key: jax.random.permutation(sub_key, TOK_DEV))(source_keys).astype(jnp.int32)
        target_order = jax.vmap(lambda sub_key: jax.random.permutation(sub_key, TOK_DEV))(target_keys).astype(jnp.int32)
        source_ids = jnp.arange(N_SEQ, dtype=jnp.int32)[:, None]
        token_ids = source_ids * TOK_DEV + source_order
        owner_ids = (source_ids + lot_of_slot[None, :]) % N_SEQ
        position = owner_ids * TOK_DEV + target_order[owner_ids, slot_index[None, :]]
        return jnp.zeros((TOKENS,), jnp.int32).at[position.reshape(-1)].set(token_ids.reshape(-1))
    return jax.vmap(one_head)(jax.random.split(base_key, HEADS))


def draw_token_perm(key, part):
    return perm_table(key)


def draw_pair_blocks(key, part):
    base_key = jax.random.fold_in(key, 202)

    def one_head(head_key):

        def one_device(device_key, device):
            offsets = jax.random.permutation(jax.random.fold_in(device_key, 1), N_SEQ - 1)[:N_SEQ // 2] + 1
            picked = jax.random.randint(jax.random.fold_in(device_key, 2), (N_SEQ // 2,), 0, BLOCKS_DEV)
            chosen = (device + offsets) % N_SEQ * BLOCKS_DEV + picked
            entry_index = (jnp.arange(BLOCKS_DEV)[:, None] * (N_SEQ // 8) + jnp.arange(LISTED_KEY_BLOCKS)[None, :]) % (N_SEQ // 2)
            return chosen[entry_index]
        device_keys = jax.random.split(head_key, N_SEQ)
        listed = jax.vmap(one_device)(device_keys, jnp.arange(N_SEQ, dtype=jnp.int32))
        return listed.reshape(HEAD_BLOCKS, LISTED_KEY_BLOCKS)
    return jax.vmap(one_head)(jax.random.split(base_key, HEADS)).astype(jnp.int32)


def key_drawn(key):
    drawn_key = jax.random.fold_in(key, 303)
    return jnp.clip(jax.random.normal(drawn_key, (TOKENS, HEADS, HEAD_SIZE), jnp.float32), -6.0, 6.0)


def draw_keys(key, part):
    table = key_drawn(key)
    return table.reshape(TOKENS, HEADS * HEAD_SIZE).astype(jnp.bfloat16)


def draw_queries(key, part):
    query_key = jax.random.fold_in(key, 505)
    table = 2.0 * jnp.clip(jax.random.normal(query_key, (TOKENS, HEADS, HEAD_SIZE), jnp.float32), -6.0, 6.0)
    return table.reshape(TOKENS, HEADS * HEAD_SIZE).astype(jnp.bfloat16)


def place_ends(result, stream_key, low, largest):
    longest = result.shape.index(max(result.shape))
    spots = []
    for shift in (0, 1):
        where = [jax.random.randint(jax.random.fold_in(stream_key, axis), (), 0, length) for axis, length in enumerate(result.shape)]
        where[longest] = (where[longest] + shift) % result.shape[longest]
        spots.append(tuple(where))
    return result.at[spots[0]].set(low).at[spots[1]].set(largest)


def steps_of(own_key, extent, pieces, smallest, largest):
    gain, own = 1.0, jax.random.fold_in(own_key, 6)
    for dim, shards_of in pieces:
        steps = jnp.exp(jax.random.uniform(jax.random.fold_in(own, dim), (shards_of,), jnp.float32, smallest / len(pieces), largest / len(pieces)))
        gain = gain * jnp.repeat(steps, extent[dim] // shards_of).reshape([-1 if axis == dim else 1 for axis in range(len(extent))])
    return gain


def normal_values(rng, shape, spread, reach, pieces=(), kind=jnp.bfloat16):
    drawn = jax.random.normal(rng, shape, jnp.float32) * spread
    if len(pieces) > 0:
        drawn = steps_of(rng, shape, pieces, -0.22, 0.18) * drawn
    return jnp.clip(drawn, min=-reach, max=reach).astype(kind)


def setup_inputs(seed: int = 0) -> dict:
    seeds = jax.random.split(jax.random.key(seed), 8)
    queries = draw_queries(jax.random.fold_in(seeds[7], 71), 0)
    keys = draw_keys(jax.random.fold_in(seeds[7], 71), 0)
    values = normal_values(seeds[2], (TOKENS, HEADS * HEAD_SIZE), 1.0, 6.0, ((0, 16), (1, 2)))
    token_perm = draw_token_perm(jax.random.fold_in(seeds[7], 71), 0)
    pair_blocks = draw_pair_blocks(jax.random.fold_in(seeds[7], 71), 0)
    pair_counts = place_ends(jax.random.randint(seeds[5], (HEADS, HEAD_BLOCKS), LISTED_KEY_BLOCKS // 2, LISTED_KEY_BLOCKS + 1), jax.random.fold_in(seeds[5], 1), LISTED_KEY_BLOCKS // 2, LISTED_KEY_BLOCKS).astype(jnp.int32)
    out_weight = normal_values(seeds[6], (HEADS * HEAD_SIZE, D), (HEADS * HEAD_SIZE // 16) ** -0.5, 0.875, ((0, 2),))
    return dict(queries=queries, keys=keys, values=values, token_perm=token_perm, pair_blocks=pair_blocks, pair_counts=pair_counts, out_weight=out_weight)


def attend_head(packed):
    query_rows, key_rows, value_rows, token_order, pair_list, live_count = packed
    logit_scale_factor = 1.0 / math.sqrt(HEAD_SIZE)
    query_reorder = query_rows[token_order].astype(jnp.float32)
    key_perm = key_rows[token_order].astype(jnp.float32)
    value_perm = value_rows[token_order].astype(jnp.float32)
    query_blocks = query_reorder.reshape(N_SEQ, BLOCKS_DEV, BLOCK_POSITIONS, HEAD_SIZE)
    home_keys = key_perm.reshape(N_SEQ, TOK_DEV, HEAD_SIZE)
    home_values = value_perm.reshape(N_SEQ, TOK_DEV, HEAD_SIZE)
    near_scores = jnp.einsum('nbqd,nkd->nbqk', query_blocks, home_keys).reshape(HEAD_BLOCKS, BLOCK_POSITIONS, TOK_DEV) * logit_scale_factor
    distant_keys = key_perm.reshape(HEAD_BLOCKS, BLOCK_POSITIONS, HEAD_SIZE)[pair_list]
    distant_values = value_perm.reshape(HEAD_BLOCKS, BLOCK_POSITIONS, HEAD_SIZE)[pair_list]
    distant_scores = jnp.einsum('nlg,nshg->nlsh', query_reorder.reshape(HEAD_BLOCKS, BLOCK_POSITIONS, HEAD_SIZE), distant_keys) * logit_scale_factor
    live_mask = jnp.arange(LISTED_KEY_BLOCKS)[None, :] < live_count[:, None]
    distant_scores = jnp.where(live_mask[:, None, :, None], distant_scores, -jnp.inf).reshape(HEAD_BLOCKS, BLOCK_POSITIONS, LISTED_KEY_BLOCKS * BLOCK_POSITIONS)
    row_max = jnp.maximum(lax.optimization_barrier(jnp.max(near_scores, axis=2)), lax.optimization_barrier(jnp.max(distant_scores, axis=2)))[..., None]
    near_exp = jnp.exp(near_scores - row_max)
    far_exp = jnp.exp(distant_scores - row_max)
    summed = lax.optimization_barrier(jnp.sum(near_exp, axis=2, keepdims=True)) + lax.optimization_barrier(jnp.sum(far_exp, axis=2, keepdims=True))
    near_probs = lax.optimization_barrier((near_exp / summed).astype(jnp.bfloat16)).astype(jnp.float32)
    distant_probabilities = lax.optimization_barrier((far_exp / summed).astype(jnp.bfloat16)).astype(jnp.float32)
    near_term = jnp.einsum('nbqk,nkd->nbqd', near_probs.reshape(N_SEQ, BLOCKS_DEV, BLOCK_POSITIONS, TOK_DEV), home_values)
    distant_partial = jnp.einsum('onfz,ofzj->onj', distant_probabilities.reshape(HEAD_BLOCKS, BLOCK_POSITIONS, LISTED_KEY_BLOCKS, BLOCK_POSITIONS), distant_values)
    attended = (near_term.reshape(HEAD_BLOCKS, BLOCK_POSITIONS, HEAD_SIZE) + distant_partial).astype(jnp.bfloat16).reshape(TOKENS, HEAD_SIZE)
    return jnp.zeros((TOKENS, HEAD_SIZE), jnp.bfloat16).at[token_order].set(attended)

def reference(queries, keys, values, token_perm, pair_blocks, pair_counts, out_weight):
    query_heads = queries.reshape(TOKENS, HEADS, HEAD_SIZE).transpose(1, 0, 2)
    key_heads = keys.reshape(TOKENS, HEADS, HEAD_SIZE).transpose(1, 0, 2)
    value_heads = values.reshape(TOKENS, HEADS, HEAD_SIZE).transpose(1, 0, 2)
    per_head = lax.map(attend_head, (query_heads, key_heads, value_heads, token_perm, pair_blocks, pair_counts))
    joined = per_head.transpose(1, 0, 2).reshape(TOKENS, HEADS * HEAD_SIZE)
    group_cols = HEADS_DEV * HEAD_SIZE
    summed = jnp.zeros((TOKENS, D), jnp.float32)
    for group_index in range(N_HEAD):
        partial_value = jnp.dot(joined[:, group_index * group_cols:(group_index + 1) * group_cols], out_weight[group_index * group_cols:(group_index + 1) * group_cols], preferred_element_type=jnp.float32)
        summed = summed + lax.optimization_barrier(partial_value.astype(jnp.bfloat16)).astype(jnp.float32)
    return summed.astype(jnp.bfloat16)
```

```python
import functools
import math

import jax
import jax.numpy as jnp
from jax import lax
from jax.experimental import pallas as pl
from jax.experimental.pallas import tpu as pltpu
from jax.sharding import PartitionSpec as P

HEAD_SIZE = 128
BLOCKS_DEV = 4


def plain_body(queries, keys, values, token_perm, pair_blocks, pair_counts, out_weight):
    tok_rows = queries.shape[0]
    heads_here = token_perm.shape[0]
    list_len = pair_blocks.shape[2]
    seq_count = lax.axis_size("seq")
    lot_size = 2 * tok_rows // seq_count
    block_rows = tok_rows // BLOCKS_DEV
    myself = lax.axis_index("seq")
    by_owner = token_perm.reshape(heads_here, seq_count, tok_rows)
    from_here = by_owner // tok_rows == myself
    lot_rank = jnp.cumsum(from_here.astype(jnp.int32), axis=2) - 1
    slot_hit = from_here[..., None] & (lot_rank[..., None] == jnp.arange(lot_size, dtype=jnp.int32))
    local_row = by_owner - myself * tok_rows
    send_row = jnp.sum(jnp.where(slot_hit, local_row[..., None], 0), axis=2)
    send_live = jnp.any(slot_hit, axis=2)
    held_tokens = lax.dynamic_slice_in_dim(token_perm, myself * tok_rows, tok_rows, axis=1)
    held_source = held_tokens // tok_rows
    source_hot = (held_source[..., None] == jnp.arange(seq_count, dtype=jnp.int32)).astype(
        jnp.int32
    )
    held_rank = jnp.sum(jnp.cumsum(source_hot, axis=1) * source_hot, axis=2) - 1
    held_flat = held_source * lot_size + held_rank
    stacked = jnp.concatenate(
        [
            queries.reshape(tok_rows, heads_here, HEAD_SIZE),
            keys.reshape(tok_rows, heads_here, HEAD_SIZE),
            values.reshape(tok_rows, heads_here, HEAD_SIZE),
        ],
        axis=2,
    ).transpose(1, 0, 2)
    outgoing = jax.vmap(lambda table, picks: table[picks])(
        stacked, send_row.reshape(heads_here, -1)
    )
    outgoing = outgoing.reshape(heads_here, seq_count, lot_size, 3 * HEAD_SIZE)
    logit_scale_factor = 1.0 / math.sqrt(HEAD_SIZE)
    arrived = lax.all_to_all(outgoing, "seq", split_axis=1, concat_axis=1, tiled=True)
    head_count = arrived.shape[0]
    arrived_flat = arrived.reshape(head_count, seq_count * lot_size, 3 * HEAD_SIZE)
    grouped = jax.vmap(lambda table, picks: table[picks])(arrived_flat, held_flat)
    query_own = grouped[..., :HEAD_SIZE]
    key_own = grouped[..., HEAD_SIZE : 2 * HEAD_SIZE]
    value_own = grouped[..., 2 * HEAD_SIZE :]
    blocks_flat = grouped[..., HEAD_SIZE:].reshape(
        head_count * BLOCKS_DEV, block_rows, 2 * HEAD_SIZE
    )
    owners = pair_blocks // BLOCKS_DEV
    head_ids = jnp.arange(head_count, dtype=jnp.int32)
    block_code = pair_blocks % BLOCKS_DEV + BLOCKS_DEV * head_ids[:, None, None]
    owner_hit = owners.reshape(head_count, -1)[:, :, None] == jnp.arange(seq_count, dtype=jnp.int32)
    wanted = jnp.max(
        jnp.where(owner_hit, block_code.reshape(head_count, -1)[:, :, None], 0), axis=1
    )
    fetched = lax.all_to_all(
        blocks_flat[lax.all_to_all(wanted.T, "seq", split_axis=0, concat_axis=0, tiled=True)],
        "seq",
        split_axis=0,
        concat_axis=0,
        tiled=True,
    )
    far_rows = fetched[owners, head_ids[:, None, None]]
    near_scores = (
        jnp.einsum("hqd,hkd->hqk", query_own, key_own, preferred_element_type=jnp.float32)
        * logit_scale_factor
    )
    query_blocks = query_own.reshape(head_count, BLOCKS_DEV, block_rows, HEAD_SIZE)
    distant_scores = (
        jnp.einsum(
            "hbqd,hbrkd->hbqrk",
            query_blocks,
            far_rows[..., :HEAD_SIZE],
            preferred_element_type=jnp.float32,
        )
        * logit_scale_factor
    )
    live_mask = jnp.arange(list_len, dtype=jnp.int32) < pair_counts[..., None]
    distant_scores = jnp.where(live_mask[:, :, None, :, None], distant_scores, -jnp.inf)
    distant_scores = distant_scores.reshape(head_count, tok_rows, list_len * block_rows)
    row_max = jnp.maximum(jnp.max(near_scores, axis=2), jnp.max(distant_scores, axis=2))[..., None]
    near_exp = jnp.exp(near_scores - row_max)
    far_exp = jnp.exp(distant_scores - row_max)
    summed = jnp.sum(near_exp, axis=2, keepdims=True) + jnp.sum(far_exp, axis=2, keepdims=True)
    near_probs = (near_exp / summed).astype(jnp.bfloat16)
    distant_probabilities = (
        (far_exp / summed)
        .astype(jnp.bfloat16)
        .reshape(head_count, BLOCKS_DEV, block_rows, list_len, block_rows)
    )
    near_term = jnp.einsum(
        "hqk,hkd->hqd", near_probs, value_own, preferred_element_type=jnp.float32
    )
    distant_partial = jnp.einsum(
        "hbqrk,hbrkd->hbqd",
        distant_probabilities,
        far_rows[..., HEAD_SIZE:],
        preferred_element_type=jnp.float32,
    )
    attended = (near_term + distant_partial.reshape(head_count, tok_rows, HEAD_SIZE)).astype(
        jnp.bfloat16
    )
    going_back = jax.vmap(
        lambda rows_in, picks: jnp.zeros((seq_count * lot_size, HEAD_SIZE), jnp.bfloat16)
        .at[picks]
        .set(rows_in)
    )(attended, held_flat)
    came_back = lax.all_to_all(
        going_back.reshape(head_count, seq_count, lot_size, HEAD_SIZE),
        "seq",
        split_axis=1,
        concat_axis=1,
        tiled=True,
    )
    came_flat = came_back.reshape(head_count, seq_count * lot_size, HEAD_SIZE)
    target = jnp.where(send_live, send_row, tok_rows).reshape(head_count, -1)
    per_head = jax.vmap(
        lambda rows_in, picks: jnp.zeros((tok_rows, HEAD_SIZE), jnp.bfloat16)
        .at[picks]
        .set(rows_in, mode="drop")
    )(came_flat, target)
    joined = per_head.transpose(1, 0, 2).reshape(tok_rows, heads_here * HEAD_SIZE)
    partial_value = jnp.dot(joined, out_weight, preferred_element_type=jnp.float32)
    return lax.psum_scatter(
        partial_value.astype(jnp.bfloat16), "head", scatter_dimension=1, tiled=True
    )


MESH = pl.DeviceIdType.MESH
NN = (((1,), (0,)), ((), ()))
NT = (((1,), (1,)), ((), ()))
ROW_PAD = 8


def matmul(a, b, dims=NN):
    return lax.dot_general(a, b, dims, preferred_element_type=jnp.float32)


def one_hot(mask):
    return jnp.where(mask, 1.0, 0.0).astype(jnp.bfloat16)


def iota(shape, axis):
    return lax.broadcasted_iota(jnp.int32, shape, axis)


def kernel(
    seq_count, heads, lot, list_len,
    q_ref, k_ref, v_ref, perm_ref, pairs_ref, counts_ref, w_ref, out_ref,
    perm_rows, code_rows, local_rows, pick, pick_t, place, place_t,
    want_out, want_in, want_s, kv_out, kv_in, q_out, q_in, own_kv,
    far_out, far_in, near_o, near_m, near_l, own_q, attended, back_out, back_in,
    joined_own, joined_other, w_own, w_other,
    sends, recvs, w_sems, j_send, j_recv, want_sem,
):
    tok = q_ref.shape[0]
    size = HEAD_SIZE
    block = tok // BLOCKS_DEV
    slots = seq_count * lot
    cols = out_ref.shape[1]
    me = lax.axis_index("seq")
    side = lax.axis_index("head")
    scale = 1.0 / math.sqrt(HEAD_SIZE)
    kv_phase, q_phase, want_phase, far_phase = 0, 1, 2, 3
    back_phase = far_phase + heads

    barrier = pltpu.get_barrier_semaphore()

    @pl.loop(1, seq_count)
    def _(k):
        pl.semaphore_signal(
            barrier, inc=1, device_id={"seq": lax.rem(me + k, seq_count)}, device_id_type=MESH
        )

    pl.semaphore_signal(barrier, inc=1, device_id={"head": 1 - side}, device_id_type=MESH)

    own_cols = pl.ds(pl.multiple_of(side * cols, 128), cols)
    other_cols = pl.ds(pl.multiple_of((1 - side) * cols, 128), cols)
    w_local = pltpu.make_async_copy(w_ref.at[:, own_cols], w_own, w_sems.at[0])
    w_local.start()

    def push(phase, k, source, target):
        dst = lax.rem(me + k, seq_count)
        return pltpu.make_async_remote_copy(
            src_ref=source.at[dst],
            dst_ref=target.at[me],
            send_sem=sends.at[phase, k],
            recv_sem=recvs.at[phase, k],
            device_id={"seq": dst},
            device_id_type=MESH,
        )

    def start_all(phase, source, target):
        @pl.loop(1, seq_count)
        def _(k):
            push(phase, k, source, target).start()

    def wait_all(phase, source, target):
        @pl.loop(1, seq_count)
        def _(k):
            push(phase, k, source, target).wait_recv()

    def sent_all(phase, source, target):
        @pl.loop(1, seq_count)
        def _(k):
            push(phase, k, source, target).wait_send()

    owner_ids = iota((seq_count, 1, 128), 0)
    head_lanes = iota((seq_count, 1, 128), 2)
    want = jnp.zeros((seq_count, 1, 128), jnp.int32)
    for h in range(heads):
        for b in range(BLOCKS_DEV):
            for r in range(list_len):
                entry = pairs_ref[h, b, r]
                owner = lax.div(entry, BLOCKS_DEV)
                code = entry - owner * BLOCKS_DEV + BLOCKS_DEV * h
                want = jnp.where((owner_ids == owner) & (head_lanes == h), code, want)
    want_out[...] = want

    perm_rows[...] = jnp.zeros_like(perm_rows)
    for o in range(seq_count):
        perm_rows[o * ROW_PAD : o * ROW_PAD + heads, :] = perm_ref[:, o * tok : (o + 1) * tok]
    before = one_hot(iota((tok, tok), 0) < iota((tok, tok), 1))
    local = perm_rows[...] - me * tok
    from_here = (local >= 0) & (local < tok)
    rank = matmul(one_hot(from_here), before)
    code_rows[...] = jnp.where(from_here, rank, -1.0)
    local_rows[...] = local.astype(jnp.float32)
    slot_ids = iota((lot, tok), 0).astype(jnp.float32)
    lane_ids = iota((lot, tok), 1).astype(jnp.float32)
    for o in range(seq_count):
        for h in range(heads):
            row = o * ROW_PAD + h
            hit = slot_ids == code_rows[row : row + 1, :]
            picked = (
                jnp.sum(
                    jnp.where(hit, local_rows[row : row + 1, :] + 1.0, 0.0), axis=1, keepdims=True
                )
                - 1.0
            )
            pick[h, o * lot : (o + 1) * lot, :] = one_hot(lane_ids == picked)

    for h in range(heads):
        hc = slice(h * size, (h + 1) * size)
        for half, ref in ((0, k_ref), (1, v_ref)):
            rows = matmul(pick[h], ref[:, hc]).astype(jnp.bfloat16)
            kv_out[:, h * lot : (h + 1) * lot, half * size : (half + 1) * size] = rows.reshape(
                seq_count, lot, size
            )

    pl.semaphore_wait(barrier, seq_count)
    start_all(want_phase, want_out, want_in)
    start_all(kv_phase, kv_out, kv_in)
    for h in range(heads):
        rows = matmul(pick[h], q_ref[:, h * size : (h + 1) * size]).astype(jnp.bfloat16)
        q_out[:, h * lot : (h + 1) * lot, :] = rows.reshape(seq_count, lot, size)
    start_all(q_phase, q_out, q_in)
    w_remote = pltpu.make_async_remote_copy(
        src_ref=w_ref.at[:, other_cols],
        dst_ref=w_other,
        send_sem=w_sems.at[1],
        recv_sem=w_sems.at[2],
        device_id={"head": 1 - side},
        device_id_type=MESH,
    )
    w_remote.start()

    mine = perm_rows[pl.ds(pl.multiple_of(me * ROW_PAD, ROW_PAD), ROW_PAD), :]
    source_ids = iota((seq_count, tok), 0)
    flats = []
    for h in range(heads):
        gap = mine[h : h + 1, :] - source_ids * tok
        hot = (gap >= 0) & (gap < tok)
        place_of = matmul(one_hot(hot), before) + (source_ids * lot).astype(jnp.float32)
        flat = jnp.sum(jnp.where(hot, place_of, 0.0), axis=0, keepdims=True)
        place_t[h] = one_hot(iota((slots, tok), 0).astype(jnp.float32) == flat)
        flats.append(flat)
    flats = jnp.concatenate(
        [jnp.broadcast_to(f, (ROW_PAD, tok)) for f in flats], axis=0
    ).T
    for h in range(heads):
        column = flats[:, h * ROW_PAD : h * ROW_PAD + 1]
        place[h] = one_hot(iota((tok, slots), 1).astype(jnp.float32) == column)
        pick_t[h] = pick[h].T
    kv_in[me] = kv_out[me]
    q_in[me] = q_out[me]

    wait_all(want_phase, want_out, want_in)
    want_in[me] = want_out[me]
    to_scalars = pltpu.make_async_copy(want_in, want_s, want_sem)
    to_scalars.start()
    to_scalars.wait()

    wait_all(kv_phase, kv_out, kv_in)
    for h in range(heads):
        lots = kv_in[:, h * lot : (h + 1) * lot, :].reshape(slots, 2 * size)
        rows = matmul(place[h], lots).astype(jnp.bfloat16)
        own_kv[h * BLOCKS_DEV : (h + 1) * BLOCKS_DEV] = rows.reshape(BLOCKS_DEV, block, 2 * size)

        @pl.loop(1, seq_count)
        def _(k):
            dst = lax.rem(me + k, seq_count)
            far_out[h, dst] = own_kv[want_s[dst, 0, h]]

        start_all(far_phase + h, far_out.at[h], far_in[h])

    wait_all(q_phase, q_out, q_in)
    for h in range(heads):
        lots = q_in[:, h * lot : (h + 1) * lot, :].reshape(slots, size)
        query = matmul(place[h], lots).astype(jnp.bfloat16)
        own_q[h] = query
        kv = own_kv[h * BLOCKS_DEV : (h + 1) * BLOCKS_DEV].reshape(tok, 2 * size)
        scores = matmul(query, kv[:, :size], NT) * scale
        top = jnp.max(scores, axis=1, keepdims=True)
        weights = jnp.exp(scores - top)
        near_m[h] = top
        near_l[h] = jnp.sum(weights, axis=1, keepdims=True)
        near_o[h] = matmul(weights.astype(jnp.bfloat16), kv[:, size:])

    far_lanes = iota((block, list_len * block), 1)
    for h in range(heads):
        wait_all(far_phase + h, far_out.at[h], far_in[h])
        for b in range(BLOCKS_DEV):
            rows = slice(b * block, (b + 1) * block)
            far = jnp.concatenate(
                [far_in[h][lax.div(pairs_ref[h, b, r], BLOCKS_DEV)] for r in range(list_len)], axis=0
            )
            scores = matmul(own_q[h, rows, :], far[:, :size], NT) * scale
            scores = jnp.where(far_lanes < counts_ref[h, b] * block, scores, -1e30)
            near_top = near_m[h, rows, :]
            top = jnp.maximum(near_top, jnp.max(scores, axis=1, keepdims=True))
            weights = jnp.exp(scores - top)
            shrink = jnp.exp(near_top - top)
            total = near_l[h, rows, :] * shrink + jnp.sum(weights, axis=1, keepdims=True)
            mixed = near_o[h, rows, :] * shrink + matmul(
                weights.astype(jnp.bfloat16), far[:, size:]
            )
            attended[rows, :] = (mixed / total).astype(jnp.bfloat16)
        back = matmul(place_t[h], attended[...]).astype(jnp.bfloat16)
        back_out[h] = back.reshape(seq_count, lot, size)
        start_all(back_phase + h, back_out.at[h], back_in.at[h])
        back_in[h, me] = back_out[h, me]

    to_other = []
    for h in range(heads):
        wait_all(back_phase + h, back_out.at[h], back_in.at[h])
        joined_own[h] = matmul(pick_t[h], back_in[h].reshape(slots, size)).astype(jnp.bfloat16)
        copy = pltpu.make_async_remote_copy(
            src_ref=joined_own.at[h],
            dst_ref=joined_other.at[h],
            send_sem=j_send.at[h],
            recv_sem=j_recv.at[h],
            device_id={"head": 1 - side},
            device_id_type=MESH,
        )
        copy.start()
        to_other.append(copy)
    w_local.wait()
    w_remote.wait_recv()
    step = 512 if cols % 512 == 0 else 128
    for copy in to_other:
        copy.wait_recv()
    left = jnp.concatenate([joined_own[h] for h in range(heads)], axis=1)
    right = jnp.concatenate([joined_other[h] for h in range(heads)], axis=1)
    for c in range(0, cols, step):
        own_part = matmul(left, w_own[:, c : c + step]).astype(jnp.bfloat16)
        other_part = matmul(right, w_other[:, c : c + step]).astype(jnp.bfloat16)
        out_ref[:, c : c + step] = (
            own_part.astype(jnp.float32) + other_part.astype(jnp.float32)
        ).astype(jnp.bfloat16)

    for copy in to_other:
        copy.wait_send()
    w_remote.wait_send()
    sent_all(want_phase, want_out, want_in)
    sent_all(kv_phase, kv_out, kv_in)
    sent_all(q_phase, q_out, q_in)
    for h in range(heads):
        sent_all(far_phase + h, far_out.at[h], far_in[h])
        sent_all(back_phase + h, back_out.at[h], back_in.at[h])


def body(queries, keys, values, token_perm, pair_blocks, pair_counts, out_weight):
    tok = queries.shape[0]
    heads = token_perm.shape[0]
    list_len = pair_blocks.shape[2]
    seq_count = lax.axis_size("seq")
    lot = 2 * tok // seq_count
    block = tok // BLOCKS_DEV
    slots = seq_count * lot
    size = HEAD_SIZE
    width = out_weight.shape[1]
    cols = width // 2
    vmem = pl.BlockSpec(memory_space=pltpu.VMEM)
    smem = pl.BlockSpec(memory_space=pltpu.SMEM)
    bf16, f32, i32 = jnp.bfloat16, jnp.float32, jnp.int32
    return pl.pallas_call(
        functools.partial(kernel, seq_count, heads, lot, list_len),
        out_shape=jax.ShapeDtypeStruct((tok, cols), bf16),
        in_specs=[vmem] * 4 + [smem] * 2 + [pl.BlockSpec(memory_space=pl.ANY)],
        out_specs=vmem,
        scratch_shapes=[
            pltpu.VMEM((seq_count * ROW_PAD, tok), i32),
            pltpu.VMEM((seq_count * ROW_PAD, tok), f32),
            pltpu.VMEM((seq_count * ROW_PAD, tok), f32),
            pltpu.VMEM((heads, slots, tok), bf16),
            pltpu.VMEM((heads, tok, slots), bf16),
            pltpu.VMEM((heads, tok, slots), bf16),
            pltpu.VMEM((heads, slots, tok), bf16),
            pltpu.VMEM((seq_count, 1, 128), i32),
            pltpu.VMEM((seq_count, 1, 128), i32),
            pltpu.SMEM((seq_count, 1, 128), i32),
            pltpu.VMEM((seq_count, heads * lot, 2 * size), bf16),
            pltpu.VMEM((seq_count, heads * lot, 2 * size), bf16),
            pltpu.VMEM((seq_count, heads * lot, size), bf16),
            pltpu.VMEM((seq_count, heads * lot, size), bf16),
            pltpu.VMEM((heads * BLOCKS_DEV, block, 2 * size), bf16),
            pltpu.VMEM((heads, seq_count, block, 2 * size), bf16),
            [pltpu.VMEM((seq_count, block, 2 * size), bf16)] * heads,
            pltpu.VMEM((heads, tok, size), f32),
            pltpu.VMEM((heads, tok, 1), f32),
            pltpu.VMEM((heads, tok, 1), f32),
            pltpu.VMEM((heads, tok, size), bf16),
            pltpu.VMEM((tok, size), bf16),
            pltpu.VMEM((heads, seq_count, lot, size), bf16),
            pltpu.VMEM((heads, seq_count, lot, size), bf16),
            pltpu.VMEM((heads, tok, size), bf16),
            pltpu.VMEM((heads, tok, size), bf16),
            pltpu.VMEM((heads * size, cols), bf16),
            pltpu.VMEM((heads * size, cols), bf16),
            pltpu.SemaphoreType.DMA((3 + 2 * heads, seq_count)),
            pltpu.SemaphoreType.DMA((3 + 2 * heads, seq_count)),
            pltpu.SemaphoreType.DMA((3,)),
            pltpu.SemaphoreType.DMA((heads,)),
            pltpu.SemaphoreType.DMA((heads,)),
            pltpu.SemaphoreType.DMA,
        ],
        compiler_params=pltpu.CompilerParams(collective_id=0, has_side_effects=True),
    )(queries, keys, values, token_perm, pair_blocks, pair_counts, out_weight)


def solution(mesh):
    placed = (
        P("seq", "head"),
        P("seq", "head"),
        P("seq", "head"),
        P("head", None),
        P("head", "seq", None),
        P("head", "seq"),
        P("head", None),
    )

    def run(queries, keys, values, token_perm, pair_blocks, pair_counts, out_weight):
        seq_count, head_groups = mesh.shape["seq"], mesh.shape["head"]
        lot = 2 * (queries.shape[0] // seq_count) // seq_count
        one = body if lot % 16 == 0 and head_groups == 2 else plain_body
        return jax.shard_map(
            one, mesh=mesh, in_specs=placed, out_specs=P("seq", "head"), check_vma=False
        )(queries, keys, values, token_perm, pair_blocks, pair_counts, out_weight)

    return run
```

```python
import functools
import math

import jax
import jax.numpy as jnp
from jax import lax
from jax.experimental import pallas as pl
from jax.experimental.pallas import tpu as pltpu
from jax.sharding import PartitionSpec as P

HEAD_SIZE = 128
BLOCKS_DEV = 4


def plain_body(queries, keys, values, token_perm, pair_blocks, pair_counts, out_weight):
    tok_rows = queries.shape[0]
    heads_here = token_perm.shape[0]
    list_len = pair_blocks.shape[2]
    seq_count = lax.axis_size("seq")
    lot_size = 2 * tok_rows // seq_count
    block_rows = tok_rows // BLOCKS_DEV
    myself = lax.axis_index("seq")
    by_owner = token_perm.reshape(heads_here, seq_count, tok_rows)
    from_here = by_owner // tok_rows == myself
    lot_rank = jnp.cumsum(from_here.astype(jnp.int32), axis=2) - 1
    slot_hit = from_here[..., None] & (lot_rank[..., None] == jnp.arange(lot_size, dtype=jnp.int32))
    local_row = by_owner - myself * tok_rows
    send_row = jnp.sum(jnp.where(slot_hit, local_row[..., None], 0), axis=2)
    send_live = jnp.any(slot_hit, axis=2)
    held_tokens = lax.dynamic_slice_in_dim(token_perm, myself * tok_rows, tok_rows, axis=1)
    held_source = held_tokens // tok_rows
    source_hot = (held_source[..., None] == jnp.arange(seq_count, dtype=jnp.int32)).astype(
        jnp.int32
    )
    held_rank = jnp.sum(jnp.cumsum(source_hot, axis=1) * source_hot, axis=2) - 1
    held_flat = held_source * lot_size + held_rank
    stacked = jnp.concatenate(
        [
            queries.reshape(tok_rows, heads_here, HEAD_SIZE),
            keys.reshape(tok_rows, heads_here, HEAD_SIZE),
            values.reshape(tok_rows, heads_here, HEAD_SIZE),
        ],
        axis=2,
    ).transpose(1, 0, 2)
    outgoing = jax.vmap(lambda table, picks: table[picks])(
        stacked, send_row.reshape(heads_here, -1)
    )
    outgoing = outgoing.reshape(heads_here, seq_count, lot_size, 3 * HEAD_SIZE)
    logit_scale_factor = 1.0 / math.sqrt(HEAD_SIZE)
    arrived = lax.all_to_all(outgoing, "seq", split_axis=1, concat_axis=1, tiled=True)
    head_count = arrived.shape[0]
    arrived_flat = arrived.reshape(head_count, seq_count * lot_size, 3 * HEAD_SIZE)
    grouped = jax.vmap(lambda table, picks: table[picks])(arrived_flat, held_flat)
    query_own = grouped[..., :HEAD_SIZE]
    key_own = grouped[..., HEAD_SIZE : 2 * HEAD_SIZE]
    value_own = grouped[..., 2 * HEAD_SIZE :]
    blocks_flat = grouped[..., HEAD_SIZE:].reshape(
        head_count * BLOCKS_DEV, block_rows, 2 * HEAD_SIZE
    )
    owners = pair_blocks // BLOCKS_DEV
    head_ids = jnp.arange(head_count, dtype=jnp.int32)
    block_code = pair_blocks % BLOCKS_DEV + BLOCKS_DEV * head_ids[:, None, None]
    owner_hit = owners.reshape(head_count, -1)[:, :, None] == jnp.arange(seq_count, dtype=jnp.int32)
    wanted = jnp.max(
        jnp.where(owner_hit, block_code.reshape(head_count, -1)[:, :, None], 0), axis=1
    )
    fetched = lax.all_to_all(
        blocks_flat[lax.all_to_all(wanted.T, "seq", split_axis=0, concat_axis=0, tiled=True)],
        "seq",
        split_axis=0,
        concat_axis=0,
        tiled=True,
    )
    far_rows = fetched[owners, head_ids[:, None, None]]
    near_scores = (
        jnp.einsum("hqd,hkd->hqk", query_own, key_own, preferred_element_type=jnp.float32)
        * logit_scale_factor
    )
    query_blocks = query_own.reshape(head_count, BLOCKS_DEV, block_rows, HEAD_SIZE)
    distant_scores = (
        jnp.einsum(
            "hbqd,hbrkd->hbqrk",
            query_blocks,
            far_rows[..., :HEAD_SIZE],
            preferred_element_type=jnp.float32,
        )
        * logit_scale_factor
    )
    live_mask = jnp.arange(list_len, dtype=jnp.int32) < pair_counts[..., None]
    distant_scores = jnp.where(live_mask[:, :, None, :, None], distant_scores, -jnp.inf)
    distant_scores = distant_scores.reshape(head_count, tok_rows, list_len * block_rows)
    row_max = jnp.maximum(jnp.max(near_scores, axis=2), jnp.max(distant_scores, axis=2))[..., None]
    near_exp = jnp.exp(near_scores - row_max)
    far_exp = jnp.exp(distant_scores - row_max)
    summed = jnp.sum(near_exp, axis=2, keepdims=True) + jnp.sum(far_exp, axis=2, keepdims=True)
    near_probs = (near_exp / summed).astype(jnp.bfloat16)
    distant_probabilities = (
        (far_exp / summed)
        .astype(jnp.bfloat16)
        .reshape(head_count, BLOCKS_DEV, block_rows, list_len, block_rows)
    )
    near_term = jnp.einsum(
        "hqk,hkd->hqd", near_probs, value_own, preferred_element_type=jnp.float32
    )
    distant_partial = jnp.einsum(
        "hbqrk,hbrkd->hbqd",
        distant_probabilities,
        far_rows[..., HEAD_SIZE:],
        preferred_element_type=jnp.float32,
    )
    attended = (near_term + distant_partial.reshape(head_count, tok_rows, HEAD_SIZE)).astype(
        jnp.bfloat16
    )
    going_back = jax.vmap(
        lambda rows_in, picks: jnp.zeros((seq_count * lot_size, HEAD_SIZE), jnp.bfloat16)
        .at[picks]
        .set(rows_in)
    )(attended, held_flat)
    came_back = lax.all_to_all(
        going_back.reshape(head_count, seq_count, lot_size, HEAD_SIZE),
        "seq",
        split_axis=1,
        concat_axis=1,
        tiled=True,
    )
    came_flat = came_back.reshape(head_count, seq_count * lot_size, HEAD_SIZE)
    target = jnp.where(send_live, send_row, tok_rows).reshape(head_count, -1)
    per_head = jax.vmap(
        lambda rows_in, picks: jnp.zeros((tok_rows, HEAD_SIZE), jnp.bfloat16)
        .at[picks]
        .set(rows_in, mode="drop")
    )(came_flat, target)
    joined = per_head.transpose(1, 0, 2).reshape(tok_rows, heads_here * HEAD_SIZE)
    partial_value = jnp.dot(joined, out_weight, preferred_element_type=jnp.float32)
    return lax.psum_scatter(
        partial_value.astype(jnp.bfloat16), "head", scatter_dimension=1, tiled=True
    )


MESH = pl.DeviceIdType.MESH
NN = (((1,), (0,)), ((), ()))
NT = (((1,), (1,)), ((), ()))
ROW_PAD = 8


def matmul(a, b, dims=NN):
    return lax.dot_general(a, b, dims, preferred_element_type=jnp.float32)


def one_hot(mask):
    return jnp.where(mask, 1.0, 0.0).astype(jnp.bfloat16)


def iota(shape, axis):
    return lax.broadcasted_iota(jnp.int32, shape, axis)


def kernel(
    seq_count, heads, lot, list_len,
    q_ref, k_ref, v_ref, perm_ref, pairs_ref, counts_ref, w_ref, out_ref,
    perm_rows, code_rows, local_rows, pick, pick_t, place, place_t,
    want_out, want_in, want_s, kv_out, kv_in, q_out, q_in, own_kv,
    far_out, far_in, near_o, near_m, near_l, own_q, attended, back_out, back_in,
    joined_own, joined_other, w_own, w_other,
    mirror_kv, sends, recvs, w_sems, j_send, j_recv, m_send, m_recv, want_sem,
):
    tok = q_ref.shape[0]
    size = HEAD_SIZE
    block = tok // BLOCKS_DEV
    slots = seq_count * lot
    cols = out_ref.shape[1]
    me = lax.axis_index("seq")
    side = lax.axis_index("head")
    scale = 1.0 / math.sqrt(HEAD_SIZE)
    kv_phase, q_phase, want_phase, far_phase = 0, 1, 2, 3
    relay_phase = far_phase + heads
    back_phase = relay_phase + heads
    half = seq_count // 2
    base = (me // half) * half
    mirror = lax.rem(me + half, seq_count)

    barrier = pltpu.get_barrier_semaphore()

    @pl.loop(1, seq_count)
    def _(k):
        pl.semaphore_signal(
            barrier, inc=1, device_id={"seq": lax.rem(me + k, seq_count)}, device_id_type=MESH
        )

    pl.semaphore_signal(barrier, inc=1, device_id={"head": 1 - side}, device_id_type=MESH)

    own_cols = pl.ds(pl.multiple_of(side * cols, 128), cols)
    other_cols = pl.ds(pl.multiple_of((1 - side) * cols, 128), cols)
    w_local = pltpu.make_async_copy(w_ref.at[:, own_cols], w_own, w_sems.at[0])
    w_local.start()

    def push(phase, k, source, target):
        dst = lax.rem(me + k, seq_count)
        return pltpu.make_async_remote_copy(
            src_ref=source.at[dst],
            dst_ref=target.at[me],
            send_sem=sends.at[phase, k],
            recv_sem=recvs.at[phase, k],
            device_id={"seq": dst},
            device_id_type=MESH,
        )

    def start_all(phase, source, target):
        @pl.loop(1, seq_count)
        def _(k):
            push(phase, k, source, target).start()

    def wait_all(phase, source, target):
        @pl.loop(1, seq_count)
        def _(k):
            push(phase, k, source, target).wait_recv()

    def sent_all(phase, source, target):
        @pl.loop(1, seq_count)
        def _(k):
            push(phase, k, source, target).wait_send()

    def push_near(phase, k, source, target, shift=0):
        dst = base + lax.rem(me - base + k, half)
        return pltpu.make_async_remote_copy(
            src_ref=source.at[lax.rem(dst + shift, seq_count)],
            dst_ref=target.at[lax.rem(me + shift, seq_count)],
            send_sem=sends.at[phase, k],
            recv_sem=recvs.at[phase, k],
            device_id={"seq": dst},
            device_id_type=MESH,
        )

    def start_near(*args):
        @pl.loop(1, half)
        def _(k):
            push_near(args[0], k, *args[1:]).start()

    def wait_near(*args):
        @pl.loop(1, half)
        def _(k):
            push_near(args[0], k, *args[1:]).wait_recv()

    def sent_near(*args):
        @pl.loop(1, half)
        def _(k):
            push_near(args[0], k, *args[1:]).wait_send()

    def to_mirror(h):
        return pltpu.make_async_remote_copy(
            src_ref=own_kv[h],
            dst_ref=mirror_kv[h],
            send_sem=m_send.at[h],
            recv_sem=m_recv.at[h],
            device_id={"seq": mirror},
            device_id_type=MESH,
        )

    owner_ids = iota((seq_count, 1, 128), 0)
    mirror_ids = jnp.where(owner_ids < half, owner_ids + half, owner_ids - half)
    head_lanes = iota((seq_count, 1, 128), 2)
    want = jnp.zeros((seq_count, 1, 128), jnp.int32)
    for h in range(heads):
        for b in range(BLOCKS_DEV):
            for r in range(list_len):
                entry = pairs_ref[h, b, r]
                owner = lax.div(entry, BLOCKS_DEV)
                code = entry - owner * BLOCKS_DEV
                want = jnp.where((owner_ids == owner) & (head_lanes == h), code, want)
                want = jnp.where((mirror_ids == owner) & (head_lanes == heads + h), code, want)
    want_out[...] = want

    perm_rows[...] = jnp.zeros_like(perm_rows)
    for o in range(seq_count):
        perm_rows[o * ROW_PAD : o * ROW_PAD + heads, :] = perm_ref[:, o * tok : (o + 1) * tok]
    before = one_hot(iota((tok, tok), 0) < iota((tok, tok), 1))
    local = perm_rows[...] - me * tok
    from_here = (local >= 0) & (local < tok)
    rank = matmul(one_hot(from_here), before)
    code_rows[...] = jnp.where(from_here, rank, -1.0)
    local_rows[...] = local.astype(jnp.float32)
    slot_ids = iota((lot, tok), 0).astype(jnp.float32)
    lane_ids = iota((lot, tok), 1).astype(jnp.float32)
    for o in range(seq_count):
        for h in range(heads):
            row = o * ROW_PAD + h
            hit = slot_ids == code_rows[row : row + 1, :]
            picked = (
                jnp.sum(
                    jnp.where(hit, local_rows[row : row + 1, :] + 1.0, 0.0), axis=1, keepdims=True
                )
                - 1.0
            )
            pick[h, o * lot : (o + 1) * lot, :] = one_hot(lane_ids == picked)

    for h in range(heads):
        hc = slice(h * size, (h + 1) * size)
        for part, ref in ((0, k_ref), (1, v_ref)):
            rows = matmul(pick[h], ref[:, hc]).astype(jnp.bfloat16)
            kv_out[:, h * lot : (h + 1) * lot, part * size : (part + 1) * size] = rows.reshape(
                seq_count, lot, size
            )

    pl.semaphore_wait(barrier, seq_count)
    start_near(want_phase, want_out, want_in)
    start_all(kv_phase, kv_out, kv_in)
    for h in range(heads):
        rows = matmul(pick[h], q_ref[:, h * size : (h + 1) * size]).astype(jnp.bfloat16)
        q_out[:, h * lot : (h + 1) * lot, :] = rows.reshape(seq_count, lot, size)
    start_all(q_phase, q_out, q_in)
    w_remote = pltpu.make_async_remote_copy(
        src_ref=w_ref.at[:, other_cols],
        dst_ref=w_other,
        send_sem=w_sems.at[1],
        recv_sem=w_sems.at[2],
        device_id={"head": 1 - side},
        device_id_type=MESH,
    )
    w_remote.start()

    mine = perm_rows[pl.ds(pl.multiple_of(me * ROW_PAD, ROW_PAD), ROW_PAD), :]
    source_ids = iota((seq_count, tok), 0)
    flats = []
    for h in range(heads):
        gap = mine[h : h + 1, :] - source_ids * tok
        hot = (gap >= 0) & (gap < tok)
        place_of = matmul(one_hot(hot), before) + (source_ids * lot).astype(jnp.float32)
        flat = jnp.sum(jnp.where(hot, place_of, 0.0), axis=0, keepdims=True)
        place_t[h] = one_hot(iota((slots, tok), 0).astype(jnp.float32) == flat)
        flats.append(flat)
    flats = jnp.concatenate(
        [jnp.broadcast_to(f, (ROW_PAD, tok)) for f in flats], axis=0
    ).T
    for h in range(heads):
        column = flats[:, h * ROW_PAD : h * ROW_PAD + 1]
        place[h] = one_hot(iota((tok, slots), 1).astype(jnp.float32) == column)
        pick_t[h] = pick[h].T
    kv_in[me] = kv_out[me]
    q_in[me] = q_out[me]

    wait_near(want_phase, want_out, want_in)
    want_in[me] = want_out[me]
    to_scalars = pltpu.make_async_copy(want_in, want_s, want_sem)
    to_scalars.start()
    to_scalars.wait()

    wait_all(kv_phase, kv_out, kv_in)
    for h in range(heads):
        lots = kv_in[:, h * lot : (h + 1) * lot, :].reshape(slots, 2 * size)
        rows = matmul(place[h], lots).astype(jnp.bfloat16)
        own_kv[h][...] = rows.reshape(BLOCKS_DEV, block, 2 * size)

        to_mirror(h).start()

        @pl.loop(1, half)
        def _(k):
            dst = base + lax.rem(me - base + k, half)
            far_out[h, dst] = own_kv[h][want_s[dst, 0, h]]

        start_near(far_phase + h, far_out.at[h], far_in[h])

    wait_all(q_phase, q_out, q_in)
    for h in range(heads):
        lots = q_in[:, h * lot : (h + 1) * lot, :].reshape(slots, size)
        query = matmul(place[h], lots).astype(jnp.bfloat16)
        own_q[h] = query
        kv = own_kv[h][...].reshape(tok, 2 * size)
        scores = matmul(query, kv[:, :size], NT) * scale
        top = jnp.max(scores, axis=1, keepdims=True)
        weights = jnp.exp(scores - top)
        near_m[h] = top
        near_l[h] = jnp.sum(weights, axis=1, keepdims=True)
        near_o[h] = matmul(weights.astype(jnp.bfloat16), kv[:, size:])

    far_lanes = iota((block, list_len * block), 1)

    def relay(h):
        to_mirror(h).wait_recv()

        @pl.loop(1, half)
        def _(k):
            dst = base + lax.rem(me - base + k, half)
            far_out[h, lax.rem(dst + half, seq_count)] = mirror_kv[h][want_s[dst, 0, heads + h]]

        start_near(relay_phase + h, far_out.at[h], far_in[h], half)
        far_in[h][mirror] = mirror_kv[h][want_s[me, 0, heads + h]]

    def attend(h):
        wait_near(far_phase + h, far_out.at[h], far_in[h])
        wait_near(relay_phase + h, far_out.at[h], far_in[h], half)
        for b in range(BLOCKS_DEV):
            rows = slice(b * block, (b + 1) * block)
            far = jnp.concatenate(
                [far_in[h][lax.div(pairs_ref[h, b, r], BLOCKS_DEV)] for r in range(list_len)], axis=0
            )
            scores = matmul(own_q[h, rows, :], far[:, :size], NT) * scale
            scores = jnp.where(far_lanes < counts_ref[h, b] * block, scores, -1e30)
            near_top = near_m[h, rows, :]
            top = jnp.maximum(near_top, jnp.max(scores, axis=1, keepdims=True))
            weights = jnp.exp(scores - top)
            shrink = jnp.exp(near_top - top)
            total = near_l[h, rows, :] * shrink + jnp.sum(weights, axis=1, keepdims=True)
            mixed = near_o[h, rows, :] * shrink + matmul(
                weights.astype(jnp.bfloat16), far[:, size:]
            )
            attended[rows, :] = (mixed / total).astype(jnp.bfloat16)
        back = matmul(place_t[h], attended[...]).astype(jnp.bfloat16)
        back_out[h] = back.reshape(seq_count, lot, size)
        start_all(back_phase + h, back_out.at[h], back_in.at[h])
        back_in[h, me] = back_out[h, me]

    for h in range(heads):
        relay(h)
        if h > 0:
            attend(h - 1)
    attend(heads - 1)

    to_other = []
    for h in range(heads):
        wait_all(back_phase + h, back_out.at[h], back_in.at[h])
        joined_own[h] = matmul(pick_t[h], back_in[h].reshape(slots, size)).astype(jnp.bfloat16)
        copy = pltpu.make_async_remote_copy(
            src_ref=joined_own.at[h],
            dst_ref=joined_other.at[h],
            send_sem=j_send.at[h],
            recv_sem=j_recv.at[h],
            device_id={"head": 1 - side},
            device_id_type=MESH,
        )
        copy.start()
        to_other.append(copy)
    w_local.wait()
    w_remote.wait_recv()
    step = 512 if cols % 512 == 0 else 128
    for copy in to_other:
        copy.wait_recv()
    left = jnp.concatenate([joined_own[h] for h in range(heads)], axis=1)
    right = jnp.concatenate([joined_other[h] for h in range(heads)], axis=1)
    for c in range(0, cols, step):
        own_part = matmul(left, w_own[:, c : c + step]).astype(jnp.bfloat16)
        other_part = matmul(right, w_other[:, c : c + step]).astype(jnp.bfloat16)
        out_ref[:, c : c + step] = (
            own_part.astype(jnp.float32) + other_part.astype(jnp.float32)
        ).astype(jnp.bfloat16)

    for copy in to_other:
        copy.wait_send()
    w_remote.wait_send()
    sent_near(want_phase, want_out, want_in)
    sent_all(kv_phase, kv_out, kv_in)
    sent_all(q_phase, q_out, q_in)
    for h in range(heads):
        to_mirror(h).wait_send()
        sent_near(far_phase + h, far_out.at[h], far_in[h])
        sent_near(relay_phase + h, far_out.at[h], far_in[h], half)
        sent_all(back_phase + h, back_out.at[h], back_in.at[h])


def body(queries, keys, values, token_perm, pair_blocks, pair_counts, out_weight):
    tok = queries.shape[0]
    heads = token_perm.shape[0]
    list_len = pair_blocks.shape[2]
    seq_count = lax.axis_size("seq")
    lot = 2 * tok // seq_count
    block = tok // BLOCKS_DEV
    slots = seq_count * lot
    size = HEAD_SIZE
    width = out_weight.shape[1]
    cols = width // 2
    vmem = pl.BlockSpec(memory_space=pltpu.VMEM)
    smem = pl.BlockSpec(memory_space=pltpu.SMEM)
    bf16, f32, i32 = jnp.bfloat16, jnp.float32, jnp.int32
    return pl.pallas_call(
        functools.partial(kernel, seq_count, heads, lot, list_len),
        out_shape=jax.ShapeDtypeStruct((tok, cols), bf16),
        in_specs=[vmem] * 4 + [smem] * 2 + [pl.BlockSpec(memory_space=pl.ANY)],
        out_specs=vmem,
        scratch_shapes=[
            pltpu.VMEM((seq_count * ROW_PAD, tok), i32),
            pltpu.VMEM((seq_count * ROW_PAD, tok), f32),
            pltpu.VMEM((seq_count * ROW_PAD, tok), f32),
            pltpu.VMEM((heads, slots, tok), bf16),
            pltpu.VMEM((heads, tok, slots), bf16),
            pltpu.VMEM((heads, tok, slots), bf16),
            pltpu.VMEM((heads, slots, tok), bf16),
            pltpu.VMEM((seq_count, 1, 128), i32),
            pltpu.VMEM((seq_count, 1, 128), i32),
            pltpu.SMEM((seq_count, 1, 128), i32),
            pltpu.VMEM((seq_count, heads * lot, 2 * size), bf16),
            pltpu.VMEM((seq_count, heads * lot, 2 * size), bf16),
            pltpu.VMEM((seq_count, heads * lot, size), bf16),
            pltpu.VMEM((seq_count, heads * lot, size), bf16),
            [pltpu.VMEM((BLOCKS_DEV, block, 2 * size), bf16)] * heads,
            pltpu.VMEM((heads, seq_count, block, 2 * size), bf16),
            [pltpu.VMEM((seq_count, block, 2 * size), bf16)] * heads,
            pltpu.VMEM((heads, tok, size), f32),
            pltpu.VMEM((heads, tok, 1), f32),
            pltpu.VMEM((heads, tok, 1), f32),
            pltpu.VMEM((heads, tok, size), bf16),
            pltpu.VMEM((tok, size), bf16),
            pltpu.VMEM((heads, seq_count, lot, size), bf16),
            pltpu.VMEM((heads, seq_count, lot, size), bf16),
            pltpu.VMEM((heads, tok, size), bf16),
            pltpu.VMEM((heads, tok, size), bf16),
            pltpu.VMEM((heads * size, cols), bf16),
            pltpu.VMEM((heads * size, cols), bf16),
            [pltpu.VMEM((BLOCKS_DEV, block, 2 * size), bf16)] * heads,
            pltpu.SemaphoreType.DMA((3 + 3 * heads, seq_count)),
            pltpu.SemaphoreType.DMA((3 + 3 * heads, seq_count)),
            pltpu.SemaphoreType.DMA((3,)),
            pltpu.SemaphoreType.DMA((heads,)),
            pltpu.SemaphoreType.DMA((heads,)),
            pltpu.SemaphoreType.DMA((heads,)),
            pltpu.SemaphoreType.DMA((heads,)),
            pltpu.SemaphoreType.DMA,
        ],
        compiler_params=pltpu.CompilerParams(collective_id=0, has_side_effects=True),
    )(queries, keys, values, token_perm, pair_blocks, pair_counts, out_weight)


def solution(mesh):
    placed = (
        P("seq", "head"),
        P("seq", "head"),
        P("seq", "head"),
        P("head", None),
        P("head", "seq", None),
        P("head", "seq"),
        P("head", None),
    )

    def run(queries, keys, values, token_perm, pair_blocks, pair_counts, out_weight):
        seq_count, head_groups = mesh.shape["seq"], mesh.shape["head"]
        lot = 2 * (queries.shape[0] // seq_count) // seq_count
        one = body if lot % 16 == 0 and head_groups == 2 else plain_body
        return jax.shard_map(
            one, mesh=mesh, in_specs=placed, out_specs=P("seq", "head"), check_vma=False
        )(queries, keys, values, token_perm, pair_blocks, pair_counts, out_weight)

    return run
```

```python
import functools
import math

import jax
import jax.numpy as jnp
from jax import lax
from jax.experimental import pallas as pl
from jax.experimental.pallas import tpu as pltpu
from jax.sharding import PartitionSpec as P

HEAD_SIZE = 128
BLOCKS_DEV = 4


def plain_body(queries, keys, values, token_perm, pair_blocks, pair_counts, out_weight):
    tok_rows = queries.shape[0]
    heads_here = token_perm.shape[0]
    list_len = pair_blocks.shape[2]
    seq_count = lax.axis_size("seq")
    lot_size = 2 * tok_rows // seq_count
    block_rows = tok_rows // BLOCKS_DEV
    myself = lax.axis_index("seq")
    by_owner = token_perm.reshape(heads_here, seq_count, tok_rows)
    from_here = by_owner // tok_rows == myself
    lot_rank = jnp.cumsum(from_here.astype(jnp.int32), axis=2) - 1
    slot_hit = from_here[..., None] & (lot_rank[..., None] == jnp.arange(lot_size, dtype=jnp.int32))
    local_row = by_owner - myself * tok_rows
    send_row = jnp.sum(jnp.where(slot_hit, local_row[..., None], 0), axis=2)
    send_live = jnp.any(slot_hit, axis=2)
    held_tokens = lax.dynamic_slice_in_dim(token_perm, myself * tok_rows, tok_rows, axis=1)
    held_source = held_tokens // tok_rows
    source_hot = (held_source[..., None] == jnp.arange(seq_count, dtype=jnp.int32)).astype(
        jnp.int32
    )
    held_rank = jnp.sum(jnp.cumsum(source_hot, axis=1) * source_hot, axis=2) - 1
    held_flat = held_source * lot_size + held_rank
    stacked = jnp.concatenate(
        [
            queries.reshape(tok_rows, heads_here, HEAD_SIZE),
            keys.reshape(tok_rows, heads_here, HEAD_SIZE),
            values.reshape(tok_rows, heads_here, HEAD_SIZE),
        ],
        axis=2,
    ).transpose(1, 0, 2)
    outgoing = jax.vmap(lambda table, picks: table[picks])(
        stacked, send_row.reshape(heads_here, -1)
    )
    outgoing = outgoing.reshape(heads_here, seq_count, lot_size, 3 * HEAD_SIZE)
    logit_scale_factor = 1.0 / math.sqrt(HEAD_SIZE)
    arrived = lax.all_to_all(outgoing, "seq", split_axis=1, concat_axis=1, tiled=True)
    head_count = arrived.shape[0]
    arrived_flat = arrived.reshape(head_count, seq_count * lot_size, 3 * HEAD_SIZE)
    grouped = jax.vmap(lambda table, picks: table[picks])(arrived_flat, held_flat)
    query_own = grouped[..., :HEAD_SIZE]
    key_own = grouped[..., HEAD_SIZE : 2 * HEAD_SIZE]
    value_own = grouped[..., 2 * HEAD_SIZE :]
    blocks_flat = grouped[..., HEAD_SIZE:].reshape(
        head_count * BLOCKS_DEV, block_rows, 2 * HEAD_SIZE
    )
    owners = pair_blocks // BLOCKS_DEV
    head_ids = jnp.arange(head_count, dtype=jnp.int32)
    block_code = pair_blocks % BLOCKS_DEV + BLOCKS_DEV * head_ids[:, None, None]
    owner_hit = owners.reshape(head_count, -1)[:, :, None] == jnp.arange(seq_count, dtype=jnp.int32)
    wanted = jnp.max(
        jnp.where(owner_hit, block_code.reshape(head_count, -1)[:, :, None], 0), axis=1
    )
    fetched = lax.all_to_all(
        blocks_flat[lax.all_to_all(wanted.T, "seq", split_axis=0, concat_axis=0, tiled=True)],
        "seq",
        split_axis=0,
        concat_axis=0,
        tiled=True,
    )
    far_rows = fetched[owners, head_ids[:, None, None]]
    near_scores = (
        jnp.einsum("hqd,hkd->hqk", query_own, key_own, preferred_element_type=jnp.float32)
        * logit_scale_factor
    )
    query_blocks = query_own.reshape(head_count, BLOCKS_DEV, block_rows, HEAD_SIZE)
    distant_scores = (
        jnp.einsum(
            "hbqd,hbrkd->hbqrk",
            query_blocks,
            far_rows[..., :HEAD_SIZE],
            preferred_element_type=jnp.float32,
        )
        * logit_scale_factor
    )
    live_mask = jnp.arange(list_len, dtype=jnp.int32) < pair_counts[..., None]
    distant_scores = jnp.where(live_mask[:, :, None, :, None], distant_scores, -jnp.inf)
    distant_scores = distant_scores.reshape(head_count, tok_rows, list_len * block_rows)
    row_max = jnp.maximum(jnp.max(near_scores, axis=2), jnp.max(distant_scores, axis=2))[..., None]
    near_exp = jnp.exp(near_scores - row_max)
    far_exp = jnp.exp(distant_scores - row_max)
    summed = jnp.sum(near_exp, axis=2, keepdims=True) + jnp.sum(far_exp, axis=2, keepdims=True)
    near_probs = (near_exp / summed).astype(jnp.bfloat16)
    distant_probabilities = (
        (far_exp / summed)
        .astype(jnp.bfloat16)
        .reshape(head_count, BLOCKS_DEV, block_rows, list_len, block_rows)
    )
    near_term = jnp.einsum(
        "hqk,hkd->hqd", near_probs, value_own, preferred_element_type=jnp.float32
    )
    distant_partial = jnp.einsum(
        "hbqrk,hbrkd->hbqd",
        distant_probabilities,
        far_rows[..., HEAD_SIZE:],
        preferred_element_type=jnp.float32,
    )
    attended = (near_term + distant_partial.reshape(head_count, tok_rows, HEAD_SIZE)).astype(
        jnp.bfloat16
    )
    going_back = jax.vmap(
        lambda rows_in, picks: jnp.zeros((seq_count * lot_size, HEAD_SIZE), jnp.bfloat16)
        .at[picks]
        .set(rows_in)
    )(attended, held_flat)
    came_back = lax.all_to_all(
        going_back.reshape(head_count, seq_count, lot_size, HEAD_SIZE),
        "seq",
        split_axis=1,
        concat_axis=1,
        tiled=True,
    )
    came_flat = came_back.reshape(head_count, seq_count * lot_size, HEAD_SIZE)
    target = jnp.where(send_live, send_row, tok_rows).reshape(head_count, -1)
    per_head = jax.vmap(
        lambda rows_in, picks: jnp.zeros((tok_rows, HEAD_SIZE), jnp.bfloat16)
        .at[picks]
        .set(rows_in, mode="drop")
    )(came_flat, target)
    joined = per_head.transpose(1, 0, 2).reshape(tok_rows, heads_here * HEAD_SIZE)
    partial_value = jnp.dot(joined, out_weight, preferred_element_type=jnp.float32)
    return lax.psum_scatter(
        partial_value.astype(jnp.bfloat16), "head", scatter_dimension=1, tiled=True
    )


MESH = pl.DeviceIdType.MESH
NN = (((1,), (0,)), ((), ()))
NT = (((1,), (1,)), ((), ()))
ROW_PAD = 8


def matmul(a, b, dims=NN):
    return lax.dot_general(a, b, dims, preferred_element_type=jnp.float32)


def one_hot(mask):
    return jnp.where(mask, 1.0, 0.0).astype(jnp.bfloat16)


def iota(shape, axis):
    return lax.broadcasted_iota(jnp.int32, shape, axis)


def kernel(
    seq_count, heads, lot, list_len,
    q_ref, k_ref, v_ref, perm_ref, pairs_ref, counts_ref, w_ref, out_ref,
    perm_rows, code_rows, local_rows, pick, pick_t, place, place_t,
    want_out, want_in, want_s, kv_out, kv_in, q_out, q_in, own_kv,
    far_out, far_in, near_o, near_m, near_l, own_q, attended, back_out, back_in,
    joined_own, joined_other, w_own, w_other,
    mirror_kv, sends, recvs, w_sems, j_send, j_recv, m_send, m_recv, want_sem,
):
    tok = q_ref.shape[0]
    size = HEAD_SIZE
    block = tok // BLOCKS_DEV
    slots = seq_count * lot
    cols = out_ref.shape[1]
    me = lax.axis_index("seq")
    side = lax.axis_index("head")
    scale = 1.0 / math.sqrt(HEAD_SIZE)
    kv_phase, q_phase, want_phase, far_phase = 0, 1, 2, 3
    relay_phase = far_phase + heads
    back_phase = relay_phase + heads
    half = seq_count // 2
    base = (me // half) * half
    mirror = lax.rem(me + half, seq_count)

    barrier = pltpu.get_barrier_semaphore()

    @pl.loop(1, seq_count)
    def _(k):
        pl.semaphore_signal(
            barrier, inc=1, device_id={"seq": lax.rem(me + k, seq_count)}, device_id_type=MESH
        )

    pl.semaphore_signal(barrier, inc=1, device_id={"head": 1 - side}, device_id_type=MESH)

    own_cols = pl.ds(pl.multiple_of(side * cols, 128), cols)
    other_cols = pl.ds(pl.multiple_of((1 - side) * cols, 128), cols)
    w_local = pltpu.make_async_copy(w_ref.at[:, own_cols], w_own, w_sems.at[0])
    w_local.start()

    def push(phase, k, source, target):
        dst = lax.rem(me + k, seq_count)
        return pltpu.make_async_remote_copy(
            src_ref=source.at[dst],
            dst_ref=target.at[me],
            send_sem=sends.at[phase, k],
            recv_sem=recvs.at[phase, k],
            device_id={"seq": dst},
            device_id_type=MESH,
        )

    def start_all(phase, source, target):
        @pl.loop(1, seq_count)
        def _(k):
            push(phase, k, source, target).start()

    def wait_all(phase, source, target):
        @pl.loop(1, seq_count)
        def _(k):
            push(phase, k, source, target).wait_recv()

    def sent_all(phase, source, target):
        @pl.loop(1, seq_count)
        def _(k):
            push(phase, k, source, target).wait_send()

    def push_near(phase, k, source, target, shift=0):
        dst = base + lax.rem(me - base + k, half)
        return pltpu.make_async_remote_copy(
            src_ref=source.at[lax.rem(dst + shift, seq_count)],
            dst_ref=target.at[lax.rem(me + shift, seq_count)],
            send_sem=sends.at[phase, k],
            recv_sem=recvs.at[phase, k],
            device_id={"seq": dst},
            device_id_type=MESH,
        )

    def start_near(*args):
        @pl.loop(1, half)
        def _(k):
            push_near(args[0], k, *args[1:]).start()

    def wait_near(*args):
        @pl.loop(1, half)
        def _(k):
            push_near(args[0], k, *args[1:]).wait_recv()

    def sent_near(*args):
        @pl.loop(1, half)
        def _(k):
            push_near(args[0], k, *args[1:]).wait_send()

    def to_mirror(h):
        return pltpu.make_async_remote_copy(
            src_ref=own_kv[h],
            dst_ref=mirror_kv[h],
            send_sem=m_send.at[h],
            recv_sem=m_recv.at[h],
            device_id={"seq": mirror},
            device_id_type=MESH,
        )

    owner_ids = iota((seq_count, 1, 128), 0)
    mirror_ids = jnp.where(owner_ids < half, owner_ids + half, owner_ids - half)
    head_lanes = iota((seq_count, 1, 128), 2)
    want = jnp.zeros((seq_count, 1, 128), jnp.int32)
    for h in range(heads):
        for b in range(BLOCKS_DEV):
            for r in range(list_len):
                entry = pairs_ref[h, b, r]
                owner = lax.div(entry, BLOCKS_DEV)
                code = entry - owner * BLOCKS_DEV
                want = jnp.where((owner_ids == owner) & (head_lanes == h), code, want)
                want = jnp.where((mirror_ids == owner) & (head_lanes == heads + h), code, want)
    want_out[...] = want

    perm_rows[...] = jnp.zeros_like(perm_rows)
    for o in range(seq_count):
        perm_rows[o * ROW_PAD : o * ROW_PAD + heads, :] = perm_ref[:, o * tok : (o + 1) * tok]
    before = one_hot(iota((tok, tok), 0) < iota((tok, tok), 1))
    local = perm_rows[...] - me * tok
    from_here = (local >= 0) & (local < tok)
    rank = matmul(one_hot(from_here), before)
    code_rows[...] = jnp.where(from_here, rank, -1.0)
    local_rows[...] = local.astype(jnp.float32)
    slot_ids = iota((lot, tok), 0).astype(jnp.float32)
    lane_ids = iota((lot, tok), 1).astype(jnp.float32)
    for o in range(seq_count):
        for h in range(heads):
            row = o * ROW_PAD + h
            hit = slot_ids == code_rows[row : row + 1, :]
            picked = (
                jnp.sum(
                    jnp.where(hit, local_rows[row : row + 1, :] + 1.0, 0.0), axis=1, keepdims=True
                )
                - 1.0
            )
            pick[h, o * lot : (o + 1) * lot, :] = one_hot(lane_ids == picked)

    for h in range(heads):
        hc = slice(h * size, (h + 1) * size)
        for part, ref in ((0, k_ref), (1, v_ref)):
            rows = matmul(pick[h], ref[:, hc]).astype(jnp.bfloat16)
            kv_out[:, h * lot : (h + 1) * lot, part * size : (part + 1) * size] = rows.reshape(
                seq_count, lot, size
            )

    pl.semaphore_wait(barrier, seq_count)
    start_near(want_phase, want_out, want_in)
    start_all(kv_phase, kv_out, kv_in)
    for h in range(heads):
        rows = matmul(pick[h], q_ref[:, h * size : (h + 1) * size]).astype(jnp.bfloat16)
        q_out[:, h * lot : (h + 1) * lot, :] = rows.reshape(seq_count, lot, size)
    start_all(q_phase, q_out, q_in)
    w_remote = pltpu.make_async_remote_copy(
        src_ref=w_ref.at[:, other_cols],
        dst_ref=w_other,
        send_sem=w_sems.at[1],
        recv_sem=w_sems.at[2],
        device_id={"head": 1 - side},
        device_id_type=MESH,
    )
    w_remote.start()

    kv_in[me] = kv_out[me]
    q_in[me] = q_out[me]
    want_in[me] = want_out[me]

    mine = perm_rows[pl.ds(pl.multiple_of(me * ROW_PAD, ROW_PAD), ROW_PAD), :]
    source_ids = iota((seq_count, tok), 0)
    flats = []
    for h in range(heads):
        gap = mine[h : h + 1, :] - source_ids * tok
        hot = (gap >= 0) & (gap < tok)
        place_of = matmul(one_hot(hot), before) + (source_ids * lot).astype(jnp.float32)
        flat = jnp.sum(jnp.where(hot, place_of, 0.0), axis=0, keepdims=True)
        place_t[h] = one_hot(iota((slots, tok), 0).astype(jnp.float32) == flat)
        flats.append(flat)
    flats = jnp.concatenate(
        [jnp.broadcast_to(f, (ROW_PAD, tok)) for f in flats], axis=0
    ).T
    for h in range(heads):
        column = flats[:, h * ROW_PAD : h * ROW_PAD + 1]
        place[h] = one_hot(iota((tok, slots), 1).astype(jnp.float32) == column)
        pick_t[h] = pick[h].T

    wait_near(want_phase, want_out, want_in)
    to_scalars = pltpu.make_async_copy(want_in, want_s, want_sem)
    to_scalars.start()
    to_scalars.wait()

    wait_all(kv_phase, kv_out, kv_in)
    for h in range(heads):
        lots = kv_in[:, h * lot : (h + 1) * lot, :].reshape(slots, 2 * size)
        rows = matmul(place[h], lots).astype(jnp.bfloat16)
        own_kv[h][...] = rows.reshape(BLOCKS_DEV, block, 2 * size)

        to_mirror(h).start()

        @pl.loop(1, half)
        def _(k):
            dst = base + lax.rem(me - base + k, half)
            far_out[h, dst] = own_kv[h][want_s[dst, 0, h]]

        start_near(far_phase + h, far_out.at[h], far_in[h])

    wait_all(q_phase, q_out, q_in)
    for h in range(heads):
        lots = q_in[:, h * lot : (h + 1) * lot, :].reshape(slots, size)
        query = matmul(place[h], lots).astype(jnp.bfloat16)
        own_q[h] = query
        kv = own_kv[h][...].reshape(tok, 2 * size)
        scores = matmul(query, kv[:, :size], NT) * scale
        top = jnp.max(scores, axis=1, keepdims=True)
        weights = jnp.exp(scores - top)
        near_m[h] = top
        near_l[h] = jnp.sum(weights, axis=1, keepdims=True)
        near_o[h] = matmul(weights.astype(jnp.bfloat16), kv[:, size:])

    far_lanes = iota((block, list_len * block), 1)

    def relay(h):
        to_mirror(h).wait_recv()

        @pl.loop(1, half)
        def _(k):
            dst = base + lax.rem(me - base + k, half)
            far_out[h, lax.rem(dst + half, seq_count)] = mirror_kv[h][want_s[dst, 0, heads + h]]

        start_near(relay_phase + h, far_out.at[h], far_in[h], half)
        far_in[h][mirror] = mirror_kv[h][want_s[me, 0, heads + h]]

    def attend(h):
        wait_near(far_phase + h, far_out.at[h], far_in[h])
        wait_near(relay_phase + h, far_out.at[h], far_in[h], half)
        for b in range(BLOCKS_DEV):
            rows = slice(b * block, (b + 1) * block)
            far = jnp.concatenate(
                [far_in[h][lax.div(pairs_ref[h, b, r], BLOCKS_DEV)] for r in range(list_len)], axis=0
            )
            scores = matmul(own_q[h, rows, :], far[:, :size], NT) * scale
            scores = jnp.where(far_lanes < counts_ref[h, b] * block, scores, -1e30)
            near_top = near_m[h, rows, :]
            top = jnp.maximum(near_top, jnp.max(scores, axis=1, keepdims=True))
            weights = jnp.exp(scores - top)
            shrink = jnp.exp(near_top - top)
            total = near_l[h, rows, :] * shrink + jnp.sum(weights, axis=1, keepdims=True)
            mixed = near_o[h, rows, :] * shrink + matmul(
                weights.astype(jnp.bfloat16), far[:, size:]
            )
            attended[rows, :] = (mixed / total).astype(jnp.bfloat16)
        back = matmul(place_t[h], attended[...]).astype(jnp.bfloat16)
        back_out[h] = back.reshape(seq_count, lot, size)
        start_all(back_phase + h, back_out.at[h], back_in.at[h])
        back_in[h, me] = back_out[h, me]

    for h in range(heads):
        relay(h)
        if h > 0:
            attend(h - 1)
    attend(heads - 1)

    to_other = []
    for h in range(heads):
        wait_all(back_phase + h, back_out.at[h], back_in.at[h])
        joined_own[h] = matmul(pick_t[h], back_in[h].reshape(slots, size)).astype(jnp.bfloat16)
        copy = pltpu.make_async_remote_copy(
            src_ref=joined_own.at[h],
            dst_ref=joined_other.at[h],
            send_sem=j_send.at[h],
            recv_sem=j_recv.at[h],
            device_id={"head": 1 - side},
            device_id_type=MESH,
        )
        copy.start()
        to_other.append(copy)
    w_local.wait()
    step = 512 if cols % 512 == 0 else 128
    left = jnp.concatenate([joined_own[h] for h in range(heads)], axis=1)
    for c in range(0, cols, step):
        out_ref[:, c : c + step] = matmul(left, w_own[:, c : c + step]).astype(jnp.bfloat16)
    w_remote.wait_recv()
    for copy in to_other:
        copy.wait_recv()
    right = jnp.concatenate([joined_other[h] for h in range(heads)], axis=1)
    for c in range(0, cols, step):
        other_part = matmul(right, w_other[:, c : c + step]).astype(jnp.bfloat16)
        own_part = out_ref[:, c : c + step].astype(jnp.float32)
        out_ref[:, c : c + step] = (own_part + other_part.astype(jnp.float32)).astype(jnp.bfloat16)

    for copy in to_other:
        copy.wait_send()
    w_remote.wait_send()
    sent_near(want_phase, want_out, want_in)
    sent_all(kv_phase, kv_out, kv_in)
    sent_all(q_phase, q_out, q_in)
    for h in range(heads):
        to_mirror(h).wait_send()
        sent_near(far_phase + h, far_out.at[h], far_in[h])
        sent_near(relay_phase + h, far_out.at[h], far_in[h], half)
        sent_all(back_phase + h, back_out.at[h], back_in.at[h])


def body(queries, keys, values, token_perm, pair_blocks, pair_counts, out_weight):
    tok = queries.shape[0]
    heads = token_perm.shape[0]
    list_len = pair_blocks.shape[2]
    seq_count = lax.axis_size("seq")
    lot = 2 * tok // seq_count
    block = tok // BLOCKS_DEV
    slots = seq_count * lot
    size = HEAD_SIZE
    width = out_weight.shape[1]
    cols = width // 2
    vmem = pl.BlockSpec(memory_space=pltpu.VMEM)
    smem = pl.BlockSpec(memory_space=pltpu.SMEM)
    bf16, f32, i32 = jnp.bfloat16, jnp.float32, jnp.int32
    return pl.pallas_call(
        functools.partial(kernel, seq_count, heads, lot, list_len),
        out_shape=jax.ShapeDtypeStruct((tok, cols), bf16),
        in_specs=[vmem] * 4 + [smem] * 2 + [pl.BlockSpec(memory_space=pl.ANY)],
        out_specs=vmem,
        scratch_shapes=[
            pltpu.VMEM((seq_count * ROW_PAD, tok), i32),
            pltpu.VMEM((seq_count * ROW_PAD, tok), f32),
            pltpu.VMEM((seq_count * ROW_PAD, tok), f32),
            pltpu.VMEM((heads, slots, tok), bf16),
            pltpu.VMEM((heads, tok, slots), bf16),
            pltpu.VMEM((heads, tok, slots), bf16),
            pltpu.VMEM((heads, slots, tok), bf16),
            pltpu.VMEM((seq_count, 1, 128), i32),
            pltpu.VMEM((seq_count, 1, 128), i32),
            pltpu.SMEM((seq_count, 1, 128), i32),
            pltpu.VMEM((seq_count, heads * lot, 2 * size), bf16),
            pltpu.VMEM((seq_count, heads * lot, 2 * size), bf16),
            pltpu.VMEM((seq_count, heads * lot, size), bf16),
            pltpu.VMEM((seq_count, heads * lot, size), bf16),
            [pltpu.VMEM((BLOCKS_DEV, block, 2 * size), bf16)] * heads,
            pltpu.VMEM((heads, seq_count, block, 2 * size), bf16),
            [pltpu.VMEM((seq_count, block, 2 * size), bf16)] * heads,
            pltpu.VMEM((heads, tok, size), f32),
            pltpu.VMEM((heads, tok, 1), f32),
            pltpu.VMEM((heads, tok, 1), f32),
            pltpu.VMEM((heads, tok, size), bf16),
            pltpu.VMEM((tok, size), bf16),
            pltpu.VMEM((heads, seq_count, lot, size), bf16),
            pltpu.VMEM((heads, seq_count, lot, size), bf16),
            pltpu.VMEM((heads, tok, size), bf16),
            pltpu.VMEM((heads, tok, size), bf16),
            pltpu.VMEM((heads * size, cols), bf16),
            pltpu.VMEM((heads * size, cols), bf16),
            [pltpu.VMEM((BLOCKS_DEV, block, 2 * size), bf16)] * heads,
            pltpu.SemaphoreType.DMA((3 + 3 * heads, seq_count)),
            pltpu.SemaphoreType.DMA((3 + 3 * heads, seq_count)),
            pltpu.SemaphoreType.DMA((3,)),
            pltpu.SemaphoreType.DMA((heads,)),
            pltpu.SemaphoreType.DMA((heads,)),
            pltpu.SemaphoreType.DMA((heads,)),
            pltpu.SemaphoreType.DMA((heads,)),
            pltpu.SemaphoreType.DMA,
        ],
        compiler_params=pltpu.CompilerParams(collective_id=0, has_side_effects=True),
    )(queries, keys, values, token_perm, pair_blocks, pair_counts, out_weight)


def solution(mesh):
    placed = (
        P("seq", "head"),
        P("seq", "head"),
        P("seq", "head"),
        P("head", None),
        P("head", "seq", None),
        P("head", "seq"),
        P("head", None),
    )

    def run(queries, keys, values, token_perm, pair_blocks, pair_counts, out_weight):
        seq_count, head_groups = mesh.shape["seq"], mesh.shape["head"]
        lot = 2 * (queries.shape[0] // seq_count) // seq_count
        one = body if lot % 16 == 0 and head_groups == 2 else plain_body
        return jax.shard_map(
            one, mesh=mesh, in_specs=placed, out_specs=P("seq", "head"), check_vma=False
        )(queries, keys, values, token_perm, pair_blocks, pair_counts, out_weight)

    return run
```
